256 devices in a mesh: tm: 4 (over y), space: 64 (over x, z, core).
Axes of the slice: x: 4, y: 4, z: 8, core: 2. Of those that a mesh axis runs over, the one named last changes fastest.
Arguments:
- anomalies: bfloat16 [16, 128, 262144], P('tm', None, 'space'), may hold values from -51 to 51
- obs_index: int32 [16, 65536], P('tm', 'space'), may hold values from 0 to 4095
- obs_weight: float32 [16, 65536], P('tm', 'space'), may hold values from 0.01 to 0.12
Outputs:
- smoothed: bfloat16 [16, 128, 262144], P('tm', None, 'space')
The draws below stay inside these ranges and needn't reach their ends.
All inputs are finite; a program needn't handle non-finite values.
Results may differ from the reference program's by a relative error of at most 0.0034.
Values sent between devices are 32-bit elements; how exact they have to be, the bound alone decides.
No kernel may reach another device: no remote copies, remote signals or barrier semaphores. Data moves between devices by JAX's collectives and lax.ppermute only.
A program may use at most 64 MiB of HBM per device.

```python
import math
import jax
import jax.numpy as jnp
from jax import lax

M = 128
CELLS = 4096
OBS_DEV = 1024
TIMES = 16
NCELLS = 262144
OBS = 65536


def mix_members(noise, key):
    order_keys = jax.random.split(key, 2 * TIMES)
    first_order = jax.vmap(lambda single_key: jax.random.permutation(single_key, M))(order_keys[:TIMES])
    second_order = jax.vmap(lambda single_key: jax.random.permutation(single_key, M))(order_keys[TIMES:])
    reorder = jax.vmap(lambda member_block, member_order: jnp.take(member_block, member_order, axis=0))
    return noise + 0.8 * reorder(noise, first_order) + 0.6 * reorder(noise, second_order)


def draw_anomalies(key, part):
    keys = jax.random.split(jax.random.fold_in(key, 11), 5)
    noise = jnp.clip(jax.random.normal(keys[0], (TIMES, M, NCELLS), jnp.float32), -5.0, 5.0)
    member_scale = jnp.exp(jax.random.uniform(keys[3], (TIMES, M, 1), jnp.float32, math.log(0.3), math.log(3.0)))
    mixed = mix_members(noise, keys[4])
    common = jnp.clip(jax.random.normal(keys[1], (TIMES, 1, NCELLS), jnp.float32), -5.0, 5.0)
    loading = 0.8 * jnp.clip(jax.random.normal(keys[2], (TIMES, M, 1), jnp.float32), -3.0, 3.0)
    return jnp.clip(member_scale * (mixed + loading * common), -51.0, 51.0).astype(jnp.bfloat16)


def draw_obs_weight(key, part):
    local_key = jax.random.fold_in(key, 23)
    tile_block = (jnp.arange(OBS) // OBS_DEV).astype(jnp.float32)
    ramp = 1.0 + 2.0 * tile_block / max(OBS // OBS_DEV - 1, 1)
    base = jnp.exp(jax.random.uniform(local_key, (TIMES, OBS), jnp.float32, math.log(0.01), math.log(0.04)))
    return (base * ramp[None, :]).astype(jnp.float32)


def plant(values, own_key, low, largest):
    longest = values.shape.index(max(values.shape))
    spots = []
    for shift in (0, 1):
        where = [jax.random.randint(jax.random.fold_in(own_key, axis), (), 0, length) for axis, length in enumerate(values.shape)]
        where[longest] = (where[longest] + shift) % values.shape[longest]
        spots.append(tuple(where))
    return values.at[spots[0]].set(low).at[spots[1]].set(largest)


def setup_inputs(seed: int = 0) -> dict:
    streams_of = jax.random.split(jax.random.key(seed), 4)
    anomalies = draw_anomalies(jax.random.fold_in(streams_of[3], 71), 0)
    obs_index = plant(jax.random.randint(streams_of[1], (TIMES, OBS), 0, CELLS), jax.random.fold_in(streams_of[1], 1), 0, CELLS - 1).astype(jnp.int32)
    obs_weight = draw_obs_weight(jax.random.fold_in(streams_of[3], 71), 0)
    return dict(anomalies=anomalies, obs_index=obs_index, obs_weight=obs_weight)


def reference(anomalies, obs_index, obs_weight):
    spread_dof = float(M - 1)
    tile_block = (jnp.arange(OBS) // OBS_DEV).astype(jnp.int32)
    global_index = (obs_index + tile_block[None, :] * CELLS).astype(jnp.int32)
    picked = jnp.take_along_axis(anomalies, jnp.broadcast_to(global_index[:, None, :], (TIMES, M, OBS)), axis=2)
    scaled = (picked.astype(jnp.float32) * obs_weight[:, None, :]).astype(jnp.bfloat16)
    wide = scaled.astype(jnp.float32)
    gram = jnp.einsum('tmo,tno->tmn', wide, wide)
    identity = jnp.eye(M, dtype=jnp.float32)
    weights = spread_dof * jnp.linalg.solve(spread_dof * identity + gram, jnp.broadcast_to(identity, gram.shape))

    def advance(running, weight_now):
        return (jnp.dot(weight_now, running, precision=lax.Precision.HIGHEST), running)
    _, chains = lax.scan(advance, identity, weights, reverse=True)

    def smooth_one(pair):
        chain_now, ensemble = pair
        return jnp.dot(chain_now.T.astype(jnp.bfloat16).astype(jnp.float32), ensemble.astype(jnp.float32), preferred_element_type=jnp.float32).astype(jnp.bfloat16)
    return lax.map(smooth_one, (chains, anomalies))
```

```python
import functools

import jax
import jax.numpy as jnp
from jax import lax
from jax.experimental import pallas as pl
from jax.experimental.pallas import tpu as pltpu
from jax.sharding import PartitionSpec as P

M = 128
HALF = 64
LANES = 128
ROWS = 136
HIGHEST = lax.Precision.HIGHEST
NN = (((1,), (0,)), ((), ()))
NT = (((1,), (1,)), ((), ()))
TN = (((0,), (0,)), ((), ()))


def exact_dot(left, right, dims=NN):
    return lax.dot_general(left, right, dims, precision=HIGHEST, preferred_element_type=jnp.float32)


def iota(shape, dim):
    return lax.broadcasted_iota(jnp.int32, shape, dim)


def fold(gram):
    near = jnp.bitwise_and(iota((HALF, M), 1) - iota((HALF, M), 0), M - 1) < HALF
    across = iota((HALF, M), 1) == iota((HALF, M), 0) + HALF
    body = jnp.where(near, gram[:HALF], gram[HALF:])
    rest = jnp.sum(jnp.where(across, gram[:HALF], 0.0), axis=0, keepdims=True)
    return body, rest


def unfold(body, rest):
    near = jnp.bitwise_and(iota((HALF, M), 1) - iota((HALF, M), 0), M - 1) < HALF
    across = iota((HALF, M), 1) == iota((HALF, M), 0) + HALF
    diag = iota((M, M), 0) == iota((M, M), 1)
    top = jnp.where(near, body, jnp.where(across, jnp.broadcast_to(rest, (HALF, M)), 0.0))
    bottom = jnp.where(near, 0.0, body)
    half = jnp.concatenate([top, bottom], axis=0)
    return half + jnp.where(diag, 0.0, half.T)


def gram_kernel(anomalies_ref, index_ref, weight_ref, keep_ref, send_ref):
    time = pl.program_id(0)
    core = lax.rem(lax.axis_index("space"), 2)
    cells = anomalies_ref.shape[2]
    blocks = cells // LANES
    index = index_ref[pl.ds(time, 1), :]
    weight = weight_ref[pl.ds(time, 1), :]
    count = index.shape[1]
    square = weight * weight
    first = square.astype(jnp.bfloat16).astype(jnp.float32)
    second = (square - first).astype(jnp.bfloat16).astype(jnp.float32)
    third = square - first - second
    high = lax.shift_right_logical(index, 7)
    low = jnp.bitwise_and(index, LANES - 1)
    in_block = iota((blocks, count), 0) == high
    rows = jnp.concatenate(
        [jnp.where(in_block, part, 0.0).astype(jnp.bfloat16) for part in (first, second, third)], axis=0
    )
    lanes = jnp.where(iota((LANES, count), 0) == low, 1.0, 0.0).astype(jnp.bfloat16)
    parts = lax.dot_general(rows, lanes, NT, preferred_element_type=jnp.float32)
    total = parts[:blocks] + parts[blocks : 2 * blocks] + parts[2 * blocks :]
    scale = jnp.sqrt(total)
    scaled = jnp.concatenate(
        [
            (
                anomalies_ref[0, :, b * LANES : (b + 1) * LANES].astype(jnp.float32) * scale[b : b + 1, :]
            ).astype(jnp.bfloat16)
            for b in range(blocks)
        ],
        axis=1,
    )
    gram = lax.dot_general(scaled, scaled, NT, preferred_element_type=jnp.float32)
    body, rest = fold(gram)

    def write(ref, second_of_pair):
        start = HALF if second_of_pair else 0
        ref[start : start + HALF, :] = body
        if second_of_pair:
            ref[M + 1 : M + 2, :] = rest
        else:
            ref[M : M + 8, :] = jnp.where(iota((8, M), 0) == 0, jnp.broadcast_to(rest, (8, M)), 0.0)

    for which in range(4):

        @pl.when((time == which) & (core == which // 2))
        def _():
            write(keep_ref, which % 2)

        @pl.when((time == which) & (core != which // 2))
        def _():
            write(send_ref, which % 2)


def gram_parts(anomalies, obs_index, obs_weight):
    times, members, cells = anomalies.shape
    part = jax.ShapeDtypeStruct((ROWS, M), jnp.float32)
    return pl.pallas_call(
        gram_kernel,
        grid=(times,),
        in_specs=[
            pl.BlockSpec((1, members, cells), lambda t: (t, 0, 0)),
            pl.BlockSpec(obs_index.shape, lambda t: (0, 0)),
            pl.BlockSpec(obs_weight.shape, lambda t: (0, 0)),
        ],
        out_specs=[pl.BlockSpec((ROWS, M), lambda t: (0, 0))] * 2,
        out_shape=[part, part],
        name="gram_parts",
    )(anomalies, obs_index, obs_weight)


def invert_halves(panels):
    lane = iota((8, LANES), 1)
    column = jnp.bitwise_and(lane, HALF - 1)
    first_lane = lane - column
    row = iota((8, LANES), 0)

    def column_of(panel, k):
        return jnp.take_along_axis(panel, first_lane + k, axis=1)

    def row_of(panel, k):
        return jnp.broadcast_to(panel[k : k + 1, :], panel.shape)

    for start in range(0, HALF, 4):
        own, offset = start // 8, start % 8
        rows = [row_of(panels[own], offset + j) for j in range(4)]
        columns = [column_of(panels[own], start + j) for j in range(4)]

        def at(i, j):
            return row_of(columns[j], offset + i)

        e11, e12, e22 = at(0, 0), at(0, 1), at(1, 1)
        f11, f12, f21, f22 = at(0, 2), at(0, 3), at(1, 2), at(1, 3)
        h11, h12, h22 = at(2, 2), at(2, 3), at(3, 3)
        d = 1.0 / (e11 * e22 - e12 * e12)
        x11, x12 = (e22 * f11 - e12 * f21) * d, (e22 * f12 - e12 * f22) * d
        x21, x22 = (e11 * f21 - e12 * f11) * d, (e11 * f22 - e12 * f12) * d
        s11 = h11 - (f11 * x11 + f21 * x21)
        s12 = h12 - (f11 * x12 + f21 * x22)
        s22 = h22 - (f12 * x12 + f22 * x22)
        g = 1.0 / (s11 * s22 - s12 * s12)
        m33, m34, m44 = s22 * g, -s12 * g, s11 * g
        m13, m14 = -(x11 * m33 + x12 * m34), -(x11 * m34 + x12 * m44)
        m23, m24 = -(x21 * m33 + x22 * m34), -(x21 * m34 + x22 * m44)
        m11 = e22 * d - (m13 * x11 + m14 * x12)
        m12 = -e12 * d - (m13 * x21 + m14 * x22)
        m22 = e11 * d - (m23 * x21 + m24 * x22)
        inverse = (
            (m11, m12, m13, m14),
            (m12, m22, m23, m24),
            (m13, m23, m33, m34),
            (m14, m24, m34, m44),
        )
        pivots = (column >= start) & (column < start + 4)
        rows = [jnp.where(pivots, jnp.where(column == start + j, 1.0, 0.0), rows[j]) for j in range(4)]
        solved = [
            (line[0] * rows[0] + line[1] * rows[1]) + (line[2] * rows[2] + line[3] * rows[3]) for line in inverse
        ]
        result = list(panels)
        for p in [(own + 1 + q) % 8 for q in range(8)]:
            out = jnp.where(pivots, 0.0, panels[p])
            for j in range(4):
                out = out - (columns[j] if p == own else column_of(panels[p], start + j)) * solved[j]
            if p == own:
                for i in range(4):
                    out = jnp.where(row == offset + i, solved[i], out)
            result[p] = out
        panels = result
    return panels


def invert_packed(packed):
    return jnp.concatenate(invert_halves([packed[8 * p : 8 * p + 8] for p in range(8)]), axis=0)


def invert_pair(pair):
    left = iota((HALF, M), 1) < HALF
    corner = iota((HALF, M), 1) == iota((HALF, M), 0) + HALF
    one, two = pair
    first = invert_packed(jnp.where(left, one[:HALF], pltpu.roll(two[:HALF], HALF, 1)))
    firsts = (first, pltpu.roll(first, HALF, 1))
    crosses = [exact_dot(g[HALF:, :HALF], f[:, :HALF]) for g, f in zip(pair, firsts)]
    schur = [g[HALF:] - exact_dot(x, g[:HALF]) for g, x in zip(pair, crosses)]
    second = invert_packed(jnp.where(left, pltpu.roll(schur[0], HALF, 1), schur[1]))
    seconds = (second, pltpu.roll(second, HALF, 1))
    inverses = []
    for f, x, s in zip(firsts, crosses, seconds):
        border = jnp.concatenate([x, jnp.zeros((HALF, HALF), jnp.float32)], axis=1) - jnp.where(corner, 1.0, 0.0)
        whole = exact_dot(border, exact_dot(s[:, :HALF], border), TN)
        inverses.append(jnp.concatenate([whole[:HALF] + jnp.where(left, f, 0.0), whole[HALF:]], axis=0))
    return inverses


def weights_kernel(parts_ref, out_ref):
    dof = float(M - 1)
    total = parts_ref[0]
    for k in range(1, parts_ref.shape[0]):
        total = total + parts_ref[k]
    diag = jnp.where(iota((M, M), 0) == iota((M, M), 1), dof, 0.0)
    pair = [
        unfold(total[HALF * k : HALF * k + HALF], total[M + k : M + k + 1]) + diag for k in range(2)
    ]
    first, second = (dof * w for w in invert_pair(pair))
    out_ref[:M, :] = second
    out_ref[M:, :] = exact_dot(first, second)


def weights_of(parts):
    return pl.pallas_call(
        weights_kernel,
        out_shape=jax.ShapeDtypeStruct((2 * M, M), jnp.float32),
        name="weights",
    )(parts)


def products_kernel(own_ref, other_ref, product_ref, factors_ref):
    core = lax.rem(lax.axis_index("space"), 2)
    own, other = own_ref[...], other_ref[...]
    early = jnp.where(core == 0, own, other)
    late = jnp.where(core == 0, other, own)
    product_ref[...] = exact_dot(early[M:], late[M:])
    factors_ref[: 2 * M, :] = late
    factors_ref[2 * M :, :] = exact_dot(early[:M], late[M:])


def products_of(own, other):
    return pl.pallas_call(
        products_kernel,
        out_shape=[
            jax.ShapeDtypeStruct((M, M), jnp.float32),
            jax.ShapeDtypeStruct((3 * M, M), jnp.float32),
        ],
        name="products",
    )(own, other)


def smooth_kernel(one_ref, two_ref, three_ref, factors_ref, anomalies_ref, out_ref, chains_ref):
    @pl.when(pl.program_id(0) == 0)
    def _():
        position = lax.axis_index("tm")
        eye = jnp.where(iota((M, M), 0) == iota((M, M), 1), 1.0, 0.0)
        later = [
            jnp.where(position + k < 4, ref[...], eye)
            for k, ref in ((1, one_ref), (2, two_ref), (3, three_ref))
        ]
        suffix = exact_dot(later[0], exact_dot(later[1], later[2]))
        chains_ref[3] = suffix.T.astype(jnp.bfloat16)
        earlier = exact_dot(factors_ref[...], suffix)
        for k in range(3):
            chains_ref[2 - k] = earlier[M * k : M * k + M].T.astype(jnp.bfloat16)

    out_ref[0] = jnp.dot(
        chains_ref[pl.program_id(0)], anomalies_ref[0], preferred_element_type=jnp.float32
    ).astype(jnp.bfloat16)


def smooth(later, factors, anomalies):
    times, members, cells = anomalies.shape
    whole = pl.BlockSpec((M, M), lambda t: (0, 0))
    block = pl.BlockSpec((1, members, cells), lambda t: (t, 0, 0))
    return pl.pallas_call(
        smooth_kernel,
        grid=(times,),
        in_specs=[whole, whole, whole, pl.BlockSpec((3 * M, M), lambda t: (0, 0)), block],
        out_specs=block,
        out_shape=jax.ShapeDtypeStruct(anomalies.shape, jnp.bfloat16),
        scratch_shapes=[pltpu.VMEM((4, M, M), jnp.bfloat16)],
        name="smooth",
    )(*later, factors, anomalies)


XS, ZS, CORES = 4, 8, 2


def place(x, z, core):
    return ((x % XS) * ZS + z % ZS) * CORES + core % CORES


def sites():
    return [(x, z, c) for x in range(XS) for z in range(ZS) for c in range(CORES)]


def per_device(anomalies, obs_index, obs_weight):
    swap = [(place(*s), place(s[0], s[1], s[2] + 1)) for s in sites()]
    keep, send = gram_parts(anomalies, obs_index, obs_weight)
    part = keep + lax.ppermute(send, "space", swap)
    around = [
        lax.ppermute(part, "space", [(place(*s), place(s[0] + k, s[1], s[2])) for s in sites()])
        for k in range(1, XS)
    ]
    part = part + around[0] + around[1] + around[2]
    groups = [[place(x, z, c) for z in range(ZS)] for x in range(XS) for c in range(CORES)]
    parts = lax.all_to_all(
        jnp.broadcast_to(part[None], (ZS, ROWS, M)), "space", 0, 0, axis_index_groups=groups, tiled=True
    )
    own = weights_of(parts)
    product, factors = products_of(own, lax.ppermute(own, "space", swap))
    later = [lax.ppermute(product, "tm", [(g, (g - k) % 4) for g in range(4)]) for k in range(1, 4)]
    return smooth(later, factors, anomalies)


def solution(mesh):
    return jax.shard_map(
        per_device,
        mesh=mesh,
        in_specs=(P("tm", None, "space"), P("tm", "space"), P("tm", "space")),
        out_specs=P("tm", None, "space"),
        check_vma=False,
    )
```

```python
import jax
import jax.numpy as jnp
from jax import lax
from jax.experimental import pallas as pl
from jax.experimental.pallas import tpu as pltpu
from jax.sharding import PartitionSpec as P

M = 128
HALF = 64
LANES = 128
ROWS = 136
HIGHEST = lax.Precision.HIGHEST
NN = (((1,), (0,)), ((), ()))
NT = (((1,), (1,)), ((), ()))
TN = (((0,), (0,)), ((), ()))


def exact_dot(left, right, dims=NN):
    return lax.dot_general(left, right, dims, precision=HIGHEST, preferred_element_type=jnp.float32)


def iota(shape, dim):
    return lax.broadcasted_iota(jnp.int32, shape, dim)


def fold(gram):
    near = jnp.bitwise_and(iota((HALF, M), 1) - iota((HALF, M), 0), M - 1) < HALF
    across = iota((HALF, M), 1) == iota((HALF, M), 0) + HALF
    body = jnp.where(near, gram[:HALF], gram[HALF:])
    rest = jnp.sum(jnp.where(across, gram[:HALF], 0.0), axis=0, keepdims=True)
    return body, rest


def unfold(body, rest):
    near = jnp.bitwise_and(iota((HALF, M), 1) - iota((HALF, M), 0), M - 1) < HALF
    across = iota((HALF, M), 1) == iota((HALF, M), 0) + HALF
    diag = iota((M, M), 0) == iota((M, M), 1)
    top = jnp.where(near, body, jnp.where(across, jnp.broadcast_to(rest, (HALF, M)), 0.0))
    bottom = jnp.where(near, 0.0, body)
    half = jnp.concatenate([top, bottom], axis=0)
    return half + jnp.where(diag, 0.0, half.T)


def cell_scales(index, weight, blocks):
    count = index.shape[1]
    square = weight * weight
    first = square.astype(jnp.bfloat16).astype(jnp.float32)
    second = (square - first).astype(jnp.bfloat16).astype(jnp.float32)
    third = square - first - second
    high = lax.shift_right_logical(index, 7)
    low = jnp.bitwise_and(index, LANES - 1)
    in_block = iota((blocks, count), 0) == high
    rows = jnp.concatenate(
        [jnp.where(in_block, part, 0.0).astype(jnp.bfloat16) for part in (first, second, third)], axis=0
    )
    lanes = jnp.where(iota((LANES, count), 0) == low, 1.0, 0.0).astype(jnp.bfloat16)
    parts = lax.dot_general(rows, lanes, NT, preferred_element_type=jnp.float32)
    return jnp.sqrt(parts[:blocks] + parts[blocks : 2 * blocks] + parts[2 * blocks :])


def write_grams(first, held_ref, index_ref, weight_ref, part_ref, arrived):
    blocks = held_ref.shape[2] // LANES
    scales = [
        cell_scales(index_ref[pl.ds(first + k, 1), :], weight_ref[pl.ds(first + k, 1), :], blocks)
        for k in range(2)
    ]
    rests = []
    for k in range(2):
        arrived(k)
        scaled = jnp.concatenate(
            [
                (
                    held_ref[first + k, :, b * LANES : (b + 1) * LANES].astype(jnp.float32)
                    * scales[k][b : b + 1, :]
                ).astype(jnp.bfloat16)
                for b in range(blocks)
            ],
            axis=1,
        )
        gram = lax.dot_general(scaled, scaled, NT, preferred_element_type=jnp.float32)
        body, rest = fold(gram)
        part_ref[HALF * k : HALF * k + HALF, :] = body
        rests.append(jnp.broadcast_to(rest, (8, M)))
    row = iota((8, M), 0)
    part_ref[M:, :] = jnp.where(row == 0, rests[0], jnp.where(row == 1, rests[1], 0.0))


def gram_other_kernel(anomalies_ref, index_ref, weight_ref, part_ref, held_ref, index_held, weight_held, sems):
    core = lax.rem(lax.axis_index("space"), 2)
    order = [2 * (1 - core), 2 * (1 - core) + 1, 2 * core, 2 * core + 1]
    small = [
        pltpu.make_async_copy(index_ref, index_held, sems.at[0]),
        pltpu.make_async_copy(weight_ref, weight_held, sems.at[1]),
    ]
    large = [
        pltpu.make_async_copy(anomalies_ref.at[t], held_ref.at[t], sems.at[2 + k]) for k, t in enumerate(order)
    ]
    for copy in small + large:
        copy.start()
    for copy in small:
        copy.wait()
    write_grams(order[0], held_ref, index_held, weight_held, part_ref, lambda k: large[k].wait())
    for copy in large[2:]:
        copy.wait()


def gram_own_kernel(held_ref, index_ref, weight_ref, part_ref):
    core = lax.rem(lax.axis_index("space"), 2)
    write_grams(2 * core, held_ref, index_ref, weight_ref, part_ref, lambda k: None)


HBM = pl.BlockSpec(memory_space=pltpu.HBM)
VMEM = pl.BlockSpec(memory_space=pltpu.VMEM)


def gram_cost(anomalies):
    times, members, cells = anomalies.shape
    return pl.CostEstimate(
        flops=times * members * members * cells, bytes_accessed=times * members * cells, transcendentals=0
    )


def gram_other(anomalies, obs_index, obs_weight):
    inputs = (anomalies, obs_index, obs_weight)
    return pl.pallas_call(
        gram_other_kernel,
        in_specs=[HBM] * 3,
        out_specs=[VMEM] * 4,
        out_shape=[
            jax.ShapeDtypeStruct((ROWS, M), jnp.float32),
            *(jax.ShapeDtypeStruct(x.shape, x.dtype) for x in inputs),
        ],
        scratch_shapes=[pltpu.SemaphoreType.DMA((6,))],
        compiler_params=pltpu.CompilerParams(vmem_limit_bytes=12 << 20),
        cost_estimate=gram_cost(anomalies),
        name="gram_other",
    )(*(pltpu.with_memory_space_constraint(x, pltpu.HBM) for x in inputs))


def gram_own(held, obs_index, obs_weight):
    return pl.pallas_call(
        gram_own_kernel,
        in_specs=[VMEM] * 3,
        out_specs=VMEM,
        out_shape=jax.ShapeDtypeStruct((ROWS, M), jnp.float32),
        compiler_params=pltpu.CompilerParams(vmem_limit_bytes=12 << 20),
        cost_estimate=gram_cost(held),
        name="gram_own",
    )(held, obs_index, obs_weight)


def invert_halves(panels):
    lane = iota((8, LANES), 1)
    column = jnp.bitwise_and(lane, HALF - 1)
    first_lane = lane - column
    row = iota((8, LANES), 0)

    def column_of(panel, k):
        return jnp.take_along_axis(panel, first_lane + k, axis=1)

    def row_of(panel, k):
        return jnp.broadcast_to(panel[k : k + 1, :], panel.shape)

    for start in range(0, HALF, 4):
        own, offset = start // 8, start % 8
        rows = [row_of(panels[own], offset + j) for j in range(4)]
        columns = [column_of(panels[own], start + j) for j in range(4)]

        def at(i, j):
            return row_of(columns[j], offset + i)

        e11, e12, e22 = at(0, 0), at(0, 1), at(1, 1)
        f11, f12, f21, f22 = at(0, 2), at(0, 3), at(1, 2), at(1, 3)
        h11, h12, h22 = at(2, 2), at(2, 3), at(3, 3)
        d = 1.0 / (e11 * e22 - e12 * e12)
        x11, x12 = (e22 * f11 - e12 * f21) * d, (e22 * f12 - e12 * f22) * d
        x21, x22 = (e11 * f21 - e12 * f11) * d, (e11 * f22 - e12 * f12) * d
        s11 = h11 - (f11 * x11 + f21 * x21)
        s12 = h12 - (f11 * x12 + f21 * x22)
        s22 = h22 - (f12 * x12 + f22 * x22)
        g = 1.0 / (s11 * s22 - s12 * s12)
        m33, m34, m44 = s22 * g, -s12 * g, s11 * g
        m13, m14 = -(x11 * m33 + x12 * m34), -(x11 * m34 + x12 * m44)
        m23, m24 = -(x21 * m33 + x22 * m34), -(x21 * m34 + x22 * m44)
        m11 = e22 * d - (m13 * x11 + m14 * x12)
        m12 = -e12 * d - (m13 * x21 + m14 * x22)
        m22 = e11 * d - (m23 * x21 + m24 * x22)
        inverse = (
            (m11, m12, m13, m14),
            (m12, m22, m23, m24),
            (m13, m23, m33, m34),
            (m14, m24, m34, m44),
        )
        pivots = (column >= start) & (column < start + 4)
        rows = [jnp.where(pivots, jnp.where(column == start + j, 1.0, 0.0), rows[j]) for j in range(4)]
        solved = [
            (line[0] * rows[0] + line[1] * rows[1]) + (line[2] * rows[2] + line[3] * rows[3]) for line in inverse
        ]
        result = list(panels)
        order = [(own + (start % 8 == 4) + q) % 8 for q in range(8)]
        spread = [
            {p: columns[j] if p == own else column_of(panels[p], start + j) for p in order} for j in range(4)
        ]
        for p in order:
            out = jnp.where(pivots, 0.0, panels[p])
            for j in range(4):
                out = out - spread[j][p] * solved[j]
            if p == own:
                for i in range(4):
                    out = jnp.where(row == offset + i, solved[i], out)
            result[p] = out
        panels = result
    return panels


def invert_packed(packed):
    return jnp.concatenate(invert_halves([packed[8 * p : 8 * p + 8] for p in range(8)]), axis=0)


def invert_pair(pair):
    left = iota((HALF, M), 1) < HALF
    corner = iota((HALF, M), 1) == iota((HALF, M), 0) + HALF
    one, two = pair
    first = invert_packed(jnp.where(left, one[:HALF], pltpu.roll(two[:HALF], HALF, 1)))
    firsts = (first, pltpu.roll(first, HALF, 1))
    crosses = [exact_dot(g[HALF:, :HALF], f[:, :HALF]) for g, f in zip(pair, firsts)]
    schur = [g[HALF:] - exact_dot(x, g[:HALF]) for g, x in zip(pair, crosses)]
    second = invert_packed(jnp.where(left, pltpu.roll(schur[0], HALF, 1), schur[1]))
    seconds = (second, pltpu.roll(second, HALF, 1))
    inverses = []
    for f, x, s in zip(firsts, crosses, seconds):
        border = jnp.concatenate([x, jnp.zeros((HALF, HALF), jnp.float32)], axis=1) - jnp.where(corner, 1.0, 0.0)
        whole = exact_dot(border, exact_dot(s[:, :HALF], border), TN)
        inverses.append(jnp.concatenate([whole[:HALF] + jnp.where(left, f, 0.0), whole[HALF:]], axis=0))
    return inverses


def weights_kernel(parts_ref, out_ref):
    dof = float(M - 1)
    total = parts_ref[0]
    for k in range(1, parts_ref.shape[0]):
        total = total + parts_ref[k]
    diag = jnp.where(iota((M, M), 0) == iota((M, M), 1), dof, 0.0)
    pair = [
        unfold(total[HALF * k : HALF * k + HALF], total[M + k : M + k + 1]) + diag for k in range(2)
    ]
    first, second = (dof * w for w in invert_pair(pair))
    out_ref[:M, :] = second
    out_ref[M:, :] = exact_dot(first, second)


def weights_of(parts):
    return pl.pallas_call(
        weights_kernel,
        out_shape=jax.ShapeDtypeStruct((2 * M, M), jnp.float32),
        compiler_params=pltpu.CompilerParams(vmem_limit_bytes=4 << 20),
        name="weights",
    )(parts)


def products_kernel(own_ref, other_ref, product_ref, factors_ref):
    core = lax.rem(lax.axis_index("space"), 2)
    own, other = own_ref[...], other_ref[...]
    early = jnp.where(core == 0, own, other)
    late = jnp.where(core == 0, other, own)
    product_ref[...] = exact_dot(early[M:], late[M:])
    factors_ref[: 2 * M, :] = late
    factors_ref[2 * M :, :] = exact_dot(early[:M], late[M:])


def products_of(own, other):
    return pl.pallas_call(
        products_kernel,
        out_shape=[
            jax.ShapeDtypeStruct((M, M), jnp.float32),
            jax.ShapeDtypeStruct((3 * M, M), jnp.float32),
        ],
        compiler_params=pltpu.CompilerParams(vmem_limit_bytes=4 << 20),
        name="products",
    )(own, other)


def smooth_kernel(one_ref, two_ref, three_ref, factors_ref, held_ref, out_ref, staged_ref, sems):
    position = lax.axis_index("tm")
    eye = jnp.where(iota((M, M), 0) == iota((M, M), 1), 1.0, 0.0)
    later = [
        jnp.where(position + k < 4, ref[...], eye) for k, ref in ((1, one_ref), (2, two_ref), (3, three_ref))
    ]
    suffix = exact_dot(later[0], exact_dot(later[1], later[2]))
    copies = []

    def write(time, chain):
        chain = chain.T.astype(jnp.bfloat16)
        width = held_ref.shape[2] // SPLIT
        for low in range(0, held_ref.shape[2], width):
            lanes = slice(low, low + width)
            staged_ref[time, :, lanes] = jnp.dot(
                chain, held_ref[time, :, lanes], preferred_element_type=jnp.float32
            ).astype(jnp.bfloat16)
            copies.append(
                pltpu.make_async_copy(
                    staged_ref.at[time, :, lanes], out_ref.at[time, :, lanes], sems.at[len(copies)]
                )
            )
            copies[-1].start()

    write(3, suffix)
    for k in range(3):
        write(2 - k, exact_dot(factors_ref[M * k : M * k + M, :], suffix))
    for copy in copies:
        copy.wait()


SPLIT = 4


def smooth(later, factors, held):
    times = held.shape[0]
    return pl.pallas_call(
        smooth_kernel,
        in_specs=[VMEM] * 5,
        out_specs=HBM,
        out_shape=jax.ShapeDtypeStruct(held.shape, held.dtype),
        scratch_shapes=[pltpu.VMEM(held.shape, held.dtype), pltpu.SemaphoreType.DMA((times * SPLIT,))],
        compiler_params=pltpu.CompilerParams(vmem_limit_bytes=16 << 20),
        name="smooth",
    )(*later, factors, held)


XS, ZS, CORES = 4, 8, 2


def place(x, z, core):
    return ((x % XS) * ZS + z % ZS) * CORES + core % CORES


def sites():
    return [(x, z, c) for x in range(XS) for z in range(ZS) for c in range(CORES)]


def per_device(anomalies, obs_index, obs_weight):
    swap = [(place(*s), place(s[0], s[1], s[2] + 1)) for s in sites()]
    send, held, index_held, weight_held = gram_other(anomalies, obs_index, obs_weight)
    received = lax.ppermute(send, "space", swap)
    keep = gram_own(held, index_held, weight_held)
    part = keep + received
    around = [
        lax.ppermute(part, "space", [(place(*s), place(s[0] + k, s[1], s[2])) for s in sites()])
        for k in range(1, XS)
    ]
    part = part + around[0] + around[1] + around[2]
    groups = [[place(x, z, c) for z in range(ZS)] for x in range(XS) for c in range(CORES)]
    parts = lax.all_to_all(
        jnp.broadcast_to(part[None], (ZS, ROWS, M)), "space", 0, 0, axis_index_groups=groups, tiled=True
    )
    own = weights_of(parts)
    product, factors = products_of(own, lax.ppermute(own, "space", swap))
    later = [lax.ppermute(product, "tm", [(g, (g - k) % 4) for g in range(4)]) for k in (1, 3, 2)]
    later = [later[0], later[2], later[1]]
    return smooth(later, factors, held)


def solution(mesh):
    return jax.shard_map(
        per_device,
        mesh=mesh,
        in_specs=(P("tm", None, "space"), P("tm", "space"), P("tm", "space")),
        out_specs=P("tm", None, "space"),
        check_vma=False,
    )
```

```python
import jax
import jax.numpy as jnp
from jax import lax
from jax.experimental import pallas as pl
from jax.experimental.pallas import tpu as pltpu
from jax.sharding import PartitionSpec as P

M = 128
HALF = 64
LANES = 128
ROWS = 136
HIGHEST = lax.Precision.HIGHEST
NN = (((1,), (0,)), ((), ()))
NT = (((1,), (1,)), ((), ()))
TN = (((0,), (0,)), ((), ()))


def exact_dot(left, right, dims=NN):
    return lax.dot_general(left, right, dims, precision=HIGHEST, preferred_element_type=jnp.float32)


def iota(shape, dim):
    return lax.broadcasted_iota(jnp.int32, shape, dim)


def fold(gram):
    near = jnp.bitwise_and(iota((HALF, M), 1) - iota((HALF, M), 0), M - 1) < HALF
    across = iota((HALF, M), 1) == iota((HALF, M), 0) + HALF
    body = jnp.where(near, gram[:HALF], gram[HALF:])
    rest = jnp.sum(jnp.where(across, gram[:HALF], 0.0), axis=0, keepdims=True)
    return body, rest


def unfold(body, rest):
    near = jnp.bitwise_and(iota((HALF, M), 1) - iota((HALF, M), 0), M - 1) < HALF
    across = iota((HALF, M), 1) == iota((HALF, M), 0) + HALF
    diag = iota((M, M), 0) == iota((M, M), 1)
    top = jnp.where(near, body, jnp.where(across, jnp.broadcast_to(rest, (HALF, M)), 0.0))
    bottom = jnp.where(near, 0.0, body)
    half = jnp.concatenate([top, bottom], axis=0)
    return half + jnp.where(diag, 0.0, half.T)


def cell_scales(index, weight, blocks):
    count = index.shape[1]
    square = weight * weight
    first = square.astype(jnp.bfloat16).astype(jnp.float32)
    second = (square - first).astype(jnp.bfloat16).astype(jnp.float32)
    third = square - first - second
    high = lax.shift_right_logical(index, 7)
    low = jnp.bitwise_and(index, LANES - 1)
    in_block = iota((blocks, count), 0) == high
    rows = jnp.concatenate(
        [jnp.where(in_block, part, 0.0).astype(jnp.bfloat16) for part in (first, second, third)], axis=0
    )
    lanes = jnp.where(iota((LANES, count), 0) == low, 1.0, 0.0).astype(jnp.bfloat16)
    parts = lax.dot_general(rows, lanes, NT, preferred_element_type=jnp.float32)
    return jnp.sqrt(parts[:blocks] + parts[blocks : 2 * blocks] + parts[2 * blocks :])


def write_grams(first, held_ref, index_ref, weight_ref, part_ref, arrived):
    blocks = held_ref.shape[2] // LANES
    scales = [
        cell_scales(index_ref[pl.ds(first + k, 1), :], weight_ref[pl.ds(first + k, 1), :], blocks)
        for k in range(2)
    ]
    rests = []
    for k in range(2):
        arrived(k)
        scaled = jnp.concatenate(
            [
                (
                    held_ref[first + k, :, b * LANES : (b + 1) * LANES].astype(jnp.float32)
                    * scales[k][b : b + 1, :]
                ).astype(jnp.bfloat16)
                for b in range(blocks)
            ],
            axis=1,
        )
        gram = lax.dot_general(scaled, scaled, NT, preferred_element_type=jnp.float32)
        body, rest = fold(gram)
        part_ref[HALF * k : HALF * k + HALF, :] = body
        rests.append(jnp.broadcast_to(rest, (8, M)))
    row = iota((8, M), 0)
    part_ref[M:, :] = jnp.where(row == 0, rests[0], jnp.where(row == 1, rests[1], 0.0))


def gram_other_kernel(anomalies_ref, index_ref, weight_ref, part_ref, held_ref, index_held, weight_held, sems):
    core = lax.rem(lax.axis_index("space"), 2)
    order = [2 * (1 - core), 2 * (1 - core) + 1, 2 * core, 2 * core + 1]
    small = [
        pltpu.make_async_copy(index_ref, index_held, sems.at[0]),
        pltpu.make_async_copy(weight_ref, weight_held, sems.at[1]),
    ]
    large = [
        pltpu.make_async_copy(anomalies_ref.at[t], held_ref.at[t], sems.at[2 + k]) for k, t in enumerate(order)
    ]
    for copy in small + large:
        copy.start()
    for copy in small:
        copy.wait()
    write_grams(order[0], held_ref, index_held, weight_held, part_ref, lambda k: large[k].wait())
    for copy in large[2:]:
        copy.wait()


def gram_own_kernel(held_ref, index_ref, weight_ref, part_ref):
    core = lax.rem(lax.axis_index("space"), 2)
    write_grams(2 * core, held_ref, index_ref, weight_ref, part_ref, lambda k: None)


HBM = pl.BlockSpec(memory_space=pltpu.HBM)
VMEM = pl.BlockSpec(memory_space=pltpu.VMEM)


def gram_cost(anomalies):
    times, members, cells = anomalies.shape
    return pl.CostEstimate(
        flops=times * members * members * cells, bytes_accessed=times * members * cells, transcendentals=0
    )


def gram_other(anomalies, obs_index, obs_weight):
    inputs = (anomalies, obs_index, obs_weight)
    return pl.pallas_call(
        gram_other_kernel,
        in_specs=[HBM] * 3,
        out_specs=[VMEM] * 4,
        out_shape=[
            jax.ShapeDtypeStruct((ROWS, M), jnp.float32),
            *(jax.ShapeDtypeStruct(x.shape, x.dtype) for x in inputs),
        ],
        scratch_shapes=[pltpu.SemaphoreType.DMA((6,))],
        compiler_params=pltpu.CompilerParams(vmem_limit_bytes=12 << 20),
        cost_estimate=gram_cost(anomalies),
        name="gram_other",
    )(*(pltpu.with_memory_space_constraint(x, pltpu.HBM) for x in inputs))


def gram_own(held, obs_index, obs_weight):
    return pl.pallas_call(
        gram_own_kernel,
        in_specs=[VMEM] * 3,
        out_specs=VMEM,
        out_shape=jax.ShapeDtypeStruct((ROWS, M), jnp.float32),
        compiler_params=pltpu.CompilerParams(vmem_limit_bytes=12 << 20),
        cost_estimate=gram_cost(held),
        name="gram_own",
    )(held, obs_index, obs_weight)


def invert_halves(panels):
    lane = iota((8, LANES), 1)
    column = jnp.bitwise_and(lane, HALF - 1)
    first_lane = lane - column
    row = iota((8, LANES), 0)

    def column_of(panel, k):
        return jnp.take_along_axis(panel, first_lane + k, axis=1)

    def row_of(panel, k):
        return jnp.broadcast_to(panel[k : k + 1, :], panel.shape)

    for start in range(0, HALF, 4):
        own, offset = start // 8, start % 8
        rows = [row_of(panels[own], offset + j) for j in range(4)]
        columns = [column_of(panels[own], start + j) for j in range(4)]

        def at(i, j):
            return row_of(columns[j], offset + i)

        e11, e12, e22 = at(0, 0), at(0, 1), at(1, 1)
        f11, f12, f21, f22 = at(0, 2), at(0, 3), at(1, 2), at(1, 3)
        h11, h12, h22 = at(2, 2), at(2, 3), at(3, 3)
        d = 1.0 / (e11 * e22 - e12 * e12)
        x11, x12 = (e22 * f11 - e12 * f21) * d, (e22 * f12 - e12 * f22) * d
        x21, x22 = (e11 * f21 - e12 * f11) * d, (e11 * f22 - e12 * f12) * d
        s11 = h11 - (f11 * x11 + f21 * x21)
        s12 = h12 - (f11 * x12 + f21 * x22)
        s22 = h22 - (f12 * x12 + f22 * x22)
        g = 1.0 / (s11 * s22 - s12 * s12)
        m33, m34, m44 = s22 * g, -s12 * g, s11 * g
        m13, m14 = -(x11 * m33 + x12 * m34), -(x11 * m34 + x12 * m44)
        m23, m24 = -(x21 * m33 + x22 * m34), -(x21 * m34 + x22 * m44)
        m11 = e22 * d - (m13 * x11 + m14 * x12)
        m12 = -e12 * d - (m13 * x21 + m14 * x22)
        m22 = e11 * d - (m23 * x21 + m24 * x22)
        inverse = (
            (m11, m12, m13, m14),
            (m12, m22, m23, m24),
            (m13, m23, m33, m34),
            (m14, m24, m34, m44),
        )
        pivots = (column >= start) & (column < start + 4)
        rows = [jnp.where(pivots, jnp.where(column == start + j, 1.0, 0.0), rows[j]) for j in range(4)]
        solved = [
            (line[0] * rows[0] + line[1] * rows[1]) + (line[2] * rows[2] + line[3] * rows[3]) for line in inverse
        ]
        result = list(panels)
        order = [(own + (start % 8 == 4) + q) % 8 for q in range(8)]
        spread = [
            {p: columns[j] if p == own else column_of(panels[p], start + j) for p in order} for j in range(4)
        ]
        for p in order:
            out = jnp.where(pivots, 0.0, panels[p])
            for j in range(4):
                out = out - spread[j][p] * solved[j]
            if p == own:
                for i in range(4):
                    out = jnp.where(row == offset + i, solved[i], out)
            result[p] = out
        panels = result
    return panels


def invert_packed(packed):
    return jnp.concatenate(invert_halves([packed[8 * p : 8 * p + 8] for p in range(8)]), axis=0)


def invert_pair(pair):
    left = iota((HALF, M), 1) < HALF
    corner = iota((HALF, M), 1) == iota((HALF, M), 0) + HALF
    one, two = pair
    first = invert_packed(jnp.where(left, one[:HALF], pltpu.roll(two[:HALF], HALF, 1)))
    firsts = (first, pltpu.roll(first, HALF, 1))
    crosses = [exact_dot(g[HALF:, :HALF], f[:, :HALF]) for g, f in zip(pair, firsts)]
    schur = [g[HALF:] - exact_dot(x, g[:HALF]) for g, x in zip(pair, crosses)]
    second = invert_packed(jnp.where(left, pltpu.roll(schur[0], HALF, 1), schur[1]))
    seconds = (second, pltpu.roll(second, HALF, 1))
    inverses = []
    for f, x, s in zip(firsts, crosses, seconds):
        border = jnp.concatenate([x, jnp.zeros((HALF, HALF), jnp.float32)], axis=1) - jnp.where(corner, 1.0, 0.0)
        whole = exact_dot(border, exact_dot(s[:, :HALF], border), TN)
        inverses.append(jnp.concatenate([whole[:HALF] + jnp.where(left, f, 0.0), whole[HALF:]], axis=0))
    return inverses


def weights_kernel(total_ref, out_ref):
    dof = float(M - 1)
    total = total_ref[...]
    diag = jnp.where(iota((M, M), 0) == iota((M, M), 1), dof, 0.0)
    pair = [
        unfold(total[HALF * k : HALF * k + HALF], total[M + k : M + k + 1]) + diag for k in range(2)
    ]
    first, second = (dof * w for w in invert_pair(pair))
    out_ref[:M, :] = second
    out_ref[M:, :] = exact_dot(first, second)


def weights_of(total):
    return pl.pallas_call(
        weights_kernel,
        out_shape=jax.ShapeDtypeStruct((2 * M, M), jnp.float32),
        compiler_params=pltpu.CompilerParams(vmem_limit_bytes=4 << 20),
        name="weights",
    )(total)


def products_kernel(own_ref, other_ref, product_ref, factors_ref):
    core = lax.rem(lax.axis_index("space"), 2)
    own, other = own_ref[...], other_ref[...]
    early = jnp.where(core == 0, own, other)
    late = jnp.where(core == 0, other, own)
    product_ref[...] = exact_dot(early[M:], late[M:])
    factors_ref[: 2 * M, :] = late
    factors_ref[2 * M :, :] = exact_dot(early[:M], late[M:])


def products_of(own, other):
    return pl.pallas_call(
        products_kernel,
        out_shape=[
            jax.ShapeDtypeStruct((M, M), jnp.float32),
            jax.ShapeDtypeStruct((3 * M, M), jnp.float32),
        ],
        compiler_params=pltpu.CompilerParams(vmem_limit_bytes=4 << 20),
        name="products",
    )(own, other)


def smooth_kernel(one_ref, two_ref, three_ref, factors_ref, held_ref, out_ref, staged_ref, sems):
    position = lax.axis_index("tm")
    eye = jnp.where(iota((M, M), 0) == iota((M, M), 1), 1.0, 0.0)
    later = [
        jnp.where(position + k < 4, ref[...], eye) for k, ref in ((1, one_ref), (2, two_ref), (3, three_ref))
    ]
    suffix = exact_dot(later[0], exact_dot(later[1], later[2]))
    copies = []

    def write(time, chain):
        chain = chain.T.astype(jnp.bfloat16)
        width = held_ref.shape[2] // SPLIT
        for low in range(0, held_ref.shape[2], width):
            lanes = slice(low, low + width)
            staged_ref[time, :, lanes] = jnp.dot(
                chain, held_ref[time, :, lanes], preferred_element_type=jnp.float32
            ).astype(jnp.bfloat16)
            copies.append(
                pltpu.make_async_copy(
                    staged_ref.at[time, :, lanes], out_ref.at[time, :, lanes], sems.at[len(copies)]
                )
            )
            copies[-1].start()

    write(3, suffix)
    for k in range(3):
        write(2 - k, exact_dot(factors_ref[M * k : M * k + M, :], suffix))
    for copy in copies:
        copy.wait()


SPLIT = 4


def smooth(later, factors, held):
    times = held.shape[0]
    return pl.pallas_call(
        smooth_kernel,
        in_specs=[VMEM] * 5,
        out_specs=HBM,
        out_shape=jax.ShapeDtypeStruct(held.shape, held.dtype),
        scratch_shapes=[pltpu.VMEM(held.shape, held.dtype), pltpu.SemaphoreType.DMA((times * SPLIT,))],
        compiler_params=pltpu.CompilerParams(vmem_limit_bytes=16 << 20),
        name="smooth",
    )(*later, factors, held)


XS, ZS, CORES = 4, 8, 2


def place(x, z, core):
    return ((x % XS) * ZS + z % ZS) * CORES + core % CORES


def sites():
    return [(x, z, c) for x in range(XS) for z in range(ZS) for c in range(CORES)]


def per_device(anomalies, obs_index, obs_weight):
    swap = [(place(*s), place(s[0], s[1], s[2] + 1)) for s in sites()]
    send, held, index_held, weight_held = gram_other(anomalies, obs_index, obs_weight)
    received = lax.ppermute(send, "space", swap)
    keep = gram_own(held, index_held, weight_held)
    part = keep + received
    for moves in (
        [lambda x, z: (x, z ^ 1)],
        [lambda x, z: (x ^ 1, z)],
        [lambda x, z: (x, z + 2), lambda x, z: (x, z + 6), lambda x, z: (x, z + 4)],
        [lambda x, z: (x ^ 2, z)],
    ):
        part = part + sum(
            lax.ppermute(part, "space", [(place(x, z, c), place(*move(x, z), c)) for x, z, c in sites()])
            for move in moves
        )
    own = weights_of(part)
    product, factors = products_of(own, lax.ppermute(own, "space", swap))
    later = [lax.ppermute(product, "tm", [(g, (g - k) % 4) for g in range(4)]) for k in (1, 3, 2)]
    later = [later[0], later[2], later[1]]
    return smooth(later, factors, held)


def solution(mesh):
    return jax.shard_map(
        per_device,
        mesh=mesh,
        in_specs=(P("tm", None, "space"), P("tm", "space"), P("tm", "space")),
        out_specs=P("tm", None, "space"),
        check_vma=False,
    )
```

```python
import jax
import jax.numpy as jnp
from jax import lax
from jax.experimental import pallas as pl
from jax.experimental.pallas import tpu as pltpu
from jax.sharding import PartitionSpec as P

M = 128
HALF = 64
LANES = 128
ROWS = 136
HIGHEST = lax.Precision.HIGHEST
NN = (((1,), (0,)), ((), ()))
NT = (((1,), (1,)), ((), ()))
TN = (((0,), (0,)), ((), ()))


def exact_dot(left, right, dims=NN):
    return lax.dot_general(left, right, dims, precision=HIGHEST, preferred_element_type=jnp.float32)


def iota(shape, dim):
    return lax.broadcasted_iota(jnp.int32, shape, dim)


def fold(gram):
    near = jnp.bitwise_and(iota((HALF, M), 1) - iota((HALF, M), 0), M - 1) < HALF
    across = iota((HALF, M), 1) == iota((HALF, M), 0) + HALF
    body = jnp.where(near, gram[:HALF], gram[HALF:])
    rest = jnp.sum(jnp.where(across, gram[:HALF], 0.0), axis=0, keepdims=True)
    return body, rest


def unfold(body, rest):
    near = jnp.bitwise_and(iota((HALF, M), 1) - iota((HALF, M), 0), M - 1) < HALF
    across = iota((HALF, M), 1) == iota((HALF, M), 0) + HALF
    diag = iota((M, M), 0) == iota((M, M), 1)
    top = jnp.where(near, body, jnp.where(across, jnp.broadcast_to(rest, (HALF, M)), 0.0))
    bottom = jnp.where(near, 0.0, body)
    half = jnp.concatenate([top, bottom], axis=0)
    return half + jnp.where(diag, 0.0, half.T)


def cell_scales(index, weight, blocks):
    count = index.shape[1]
    square = weight * weight
    first = square.astype(jnp.bfloat16).astype(jnp.float32)
    second = (square - first).astype(jnp.bfloat16).astype(jnp.float32)
    third = square - first - second
    high = lax.shift_right_logical(index, 7)
    low = jnp.bitwise_and(index, LANES - 1)
    in_block = iota((blocks, count), 0) == high
    rows = jnp.concatenate(
        [jnp.where(in_block, part, 0.0).astype(jnp.bfloat16) for part in (first, second, third)], axis=0
    )
    lanes = jnp.where(iota((LANES, count), 0) == low, 1.0, 0.0).astype(jnp.bfloat16)
    parts = lax.dot_general(rows, lanes, NT, preferred_element_type=jnp.float32)
    return jnp.sqrt(parts[:blocks] + parts[blocks : 2 * blocks] + parts[2 * blocks :])


def write_grams(first, held_ref, index_ref, weight_ref, part_ref, arrived):
    blocks = held_ref.shape[2] // LANES
    scales = [
        cell_scales(index_ref[pl.ds(first + k, 1), :], weight_ref[pl.ds(first + k, 1), :], blocks)
        for k in range(2)
    ]
    rests = []
    for k in range(2):
        arrived(k)
        scaled = jnp.concatenate(
            [
                (
                    held_ref[first + k, :, b * LANES : (b + 1) * LANES].astype(jnp.float32)
                    * scales[k][b : b + 1, :]
                ).astype(jnp.bfloat16)
                for b in range(blocks)
            ],
            axis=1,
        )
        gram = lax.dot_general(scaled, scaled, NT, preferred_element_type=jnp.float32)
        body, rest = fold(gram)
        part_ref[HALF * k : HALF * k + HALF, :] = body
        rests.append(jnp.broadcast_to(rest, (8, M)))
    row = iota((8, M), 0)
    part_ref[M:, :] = jnp.where(row == 0, rests[0], jnp.where(row == 1, rests[1], 0.0))


def gram_other_kernel(anomalies_ref, index_ref, weight_ref, part_ref, held_ref, index_held, weight_held, sems):
    core = lax.rem(lax.axis_index("space"), 2)
    order = [2 * (1 - core), 2 * (1 - core) + 1, 2 * core, 2 * core + 1]
    small = [
        pltpu.make_async_copy(index_ref, index_held, sems.at[0]),
        pltpu.make_async_copy(weight_ref, weight_held, sems.at[1]),
    ]
    large = [
        pltpu.make_async_copy(anomalies_ref.at[t], held_ref.at[t], sems.at[2 + k]) for k, t in enumerate(order)
    ]
    for copy in small + large:
        copy.start()
    for copy in small:
        copy.wait()
    write_grams(order[0], held_ref, index_held, weight_held, part_ref, lambda k: large[k].wait())
    for copy in large[2:]:
        copy.wait()


def gram_own_kernel(held_ref, index_ref, weight_ref, part_ref):
    core = lax.rem(lax.axis_index("space"), 2)
    write_grams(2 * core, held_ref, index_ref, weight_ref, part_ref, lambda k: None)


HBM = pl.BlockSpec(memory_space=pltpu.HBM)
VMEM = pl.BlockSpec(memory_space=pltpu.VMEM)


def gram_cost(anomalies):
    times, members, cells = anomalies.shape
    return pl.CostEstimate(
        flops=times * members * members * cells, bytes_accessed=times * members * cells, transcendentals=0
    )


def gram_other(anomalies, obs_index, obs_weight):
    inputs = (anomalies, obs_index, obs_weight)
    return pl.pallas_call(
        gram_other_kernel,
        in_specs=[HBM] * 3,
        out_specs=[VMEM] * 4,
        out_shape=[
            jax.ShapeDtypeStruct((ROWS, M), jnp.float32),
            *(jax.ShapeDtypeStruct(x.shape, x.dtype) for x in inputs),
        ],
        scratch_shapes=[pltpu.SemaphoreType.DMA((6,))],
        compiler_params=pltpu.CompilerParams(vmem_limit_bytes=12 << 20),
        cost_estimate=gram_cost(anomalies),
        name="gram_other",
    )(*(pltpu.with_memory_space_constraint(x, pltpu.HBM) for x in inputs))


def gram_own(held, obs_index, obs_weight):
    return pl.pallas_call(
        gram_own_kernel,
        in_specs=[VMEM] * 3,
        out_specs=VMEM,
        out_shape=jax.ShapeDtypeStruct((ROWS, M), jnp.float32),
        compiler_params=pltpu.CompilerParams(vmem_limit_bytes=12 << 20),
        cost_estimate=gram_cost(held),
        name="gram_own",
    )(held, obs_index, obs_weight)


def invert_four(at):
    e11, e12, e22 = at(0, 0), at(0, 1), at(1, 1)
    f11, f12, f21, f22 = at(0, 2), at(0, 3), at(1, 2), at(1, 3)
    h11, h12, h22 = at(2, 2), at(2, 3), at(3, 3)
    d = 1.0 / (e11 * e22 - e12 * e12)
    x11, x12 = (e22 * f11 - e12 * f21) * d, (e22 * f12 - e12 * f22) * d
    x21, x22 = (e11 * f21 - e12 * f11) * d, (e11 * f22 - e12 * f12) * d
    s11 = h11 - (f11 * x11 + f21 * x21)
    s12 = h12 - (f11 * x12 + f21 * x22)
    s22 = h22 - (f12 * x12 + f22 * x22)
    g = 1.0 / (s11 * s22 - s12 * s12)
    m33, m34, m44 = s22 * g, -s12 * g, s11 * g
    m13, m14 = -(x11 * m33 + x12 * m34), -(x11 * m34 + x12 * m44)
    m23, m24 = -(x21 * m33 + x22 * m34), -(x21 * m34 + x22 * m44)
    m11 = e22 * d - (m13 * x11 + m14 * x12)
    m12 = -e12 * d - (m13 * x21 + m14 * x22)
    m22 = e11 * d - (m23 * x21 + m24 * x22)
    return (
        (m11, m12, m13, m14),
        (m12, m22, m23, m24),
        (m13, m23, m33, m34),
        (m14, m24, m34, m44),
    )


def weighted(line, values):
    return (line[0] * values[0] + line[1] * values[1]) + (line[2] * values[2] + line[3] * values[3])


def invert_halves(panels):
    lane = iota((8, LANES), 1)
    column = jnp.bitwise_and(lane, HALF - 1)
    first_lane = lane - column
    row = iota((8, LANES), 0)

    def column_of(panel, k):
        return jnp.take_along_axis(panel, first_lane + k, axis=1)

    def row_of(panel, k):
        return jnp.broadcast_to(panel[k : k + 1, :], panel.shape)

    def solve(panel, start, offset, inverse):
        pivots = (column >= start) & (column < start + 4)
        rows = [
            jnp.where(pivots, jnp.where(column == start + j, 1.0, 0.0), row_of(panel, offset + j)) for j in range(4)
        ]
        return pivots, [weighted(line, rows) for line in inverse]

    def eliminate(panel, pivots, columns, solved):
        out = jnp.where(pivots, 0.0, panel)
        return out - weighted(columns, solved)

    def place_rows(panel, offset, solved):
        for i in range(4):
            panel = jnp.where(row == offset + i, solved[i], panel)
        return panel

    count = len(panels)
    for own in range(count):
        start = 8 * own
        columns = [column_of(panels[own], start + k) for k in range(8)]
        inverse = invert_four(lambda i, j: row_of(columns[j], i))
        pivots, solved = solve(panels[own], start, 0, inverse)
        ahead = [
            [weighted(line, [row_of(columns[k], l) for l in range(4)]) for line in inverse] for k in range(4, 8)
        ]
        later = [columns[4 + k] - weighted(columns[:4], ahead[k]) for k in range(4)]
        second = invert_four(lambda i, j: row_of(later[j], 4 + i))
        current = place_rows(eliminate(panels[own], pivots, columns[:4], solved), 0, solved)
        pivots_two, solved_two = solve(current, start + 4, 4, second)
        result = list(panels)
        for p in [(own + 1 + q) % count for q in range(count - 1)]:
            near = [column_of(panels[p], start + j) for j in range(4)]
            far = [column_of(panels[p], start + 4 + k) - weighted(near, ahead[k]) for k in range(4)]
            out = eliminate(panels[p], pivots, near, solved)
            result[p] = eliminate(out, pivots_two, far, solved_two)
        far = [column_of(current, start + 4 + k) for k in range(4)]
        result[own] = place_rows(eliminate(current, pivots_two, far, solved_two), 4, solved_two)
        panels = result
    return panels


def invert_packed(packed):
    return jnp.concatenate(invert_halves([packed[8 * p : 8 * p + 8] for p in range(8)]), axis=0)


def invert_pair(pair):
    left = iota((HALF, M), 1) < HALF
    corner = iota((HALF, M), 1) == iota((HALF, M), 0) + HALF
    one, two = pair
    first = invert_packed(jnp.where(left, one[:HALF], pltpu.roll(two[:HALF], HALF, 1)))
    firsts = (first, pltpu.roll(first, HALF, 1))
    crosses = [exact_dot(g[HALF:, :HALF], f[:, :HALF]) for g, f in zip(pair, firsts)]
    schur = [g[HALF:] - exact_dot(x, g[:HALF]) for g, x in zip(pair, crosses)]
    changes = [exact_dot(s[:, :HALF], f[:, :HALF]) for s, f in zip(schur, firsts)]
    schur = [s - exact_dot(x, g[:HALF]) for s, x, g in zip(schur, changes, pair)]
    crosses = [x + change for x, change in zip(crosses, changes)]
    second = invert_packed(jnp.where(left, pltpu.roll(schur[0], HALF, 1), schur[1]))
    seconds = (second, pltpu.roll(second, HALF, 1))
    inverses = []
    for f, x, s in zip(firsts, crosses, seconds):
        border = jnp.concatenate([x, jnp.zeros((HALF, HALF), jnp.float32)], axis=1) - jnp.where(corner, 1.0, 0.0)
        whole = exact_dot(border, exact_dot(s[:, :HALF], border), TN)
        inverses.append(jnp.concatenate([whole[:HALF] + jnp.where(left, f, 0.0), whole[HALF:]], axis=0))
    return inverses


def weights_kernel(total_ref, out_ref):
    dof = float(M - 1)
    total = total_ref[...]
    diag = jnp.where(iota((M, M), 0) == iota((M, M), 1), dof, 0.0)
    pair = [
        unfold(total[HALF * k : HALF * k + HALF], total[M + k : M + k + 1]) + diag for k in range(2)
    ]
    first, second = (dof * w for w in invert_pair(pair))
    out_ref[:M, :] = second
    out_ref[M:, :] = exact_dot(first, second)


def weights_of(total):
    return pl.pallas_call(
        weights_kernel,
        out_shape=jax.ShapeDtypeStruct((2 * M, M), jnp.float32),
        compiler_params=pltpu.CompilerParams(vmem_limit_bytes=4 << 20),
        name="weights",
    )(total)


def products_kernel(own_ref, other_ref, product_ref, factors_ref):
    core = lax.rem(lax.axis_index("space"), 2)
    own, other = own_ref[...], other_ref[...]
    early = jnp.where(core == 0, own, other)
    late = jnp.where(core == 0, other, own)
    product_ref[...] = exact_dot(early[M:], late[M:])
    factors_ref[: 2 * M, :] = late
    factors_ref[2 * M :, :] = exact_dot(early[:M], late[M:])


def products_of(own, other):
    return pl.pallas_call(
        products_kernel,
        out_shape=[
            jax.ShapeDtypeStruct((M, M), jnp.float32),
            jax.ShapeDtypeStruct((3 * M, M), jnp.float32),
        ],
        compiler_params=pltpu.CompilerParams(vmem_limit_bytes=4 << 20),
        name="products",
    )(own, other)


def smooth_kernel(one_ref, two_ref, three_ref, factors_ref, held_ref, out_ref, staged_ref, sems):
    position = lax.axis_index("tm")
    eye = jnp.where(iota((M, M), 0) == iota((M, M), 1), 1.0, 0.0)
    later = [
        jnp.where(position + k < 4, ref[...], eye) for k, ref in ((1, one_ref), (2, two_ref), (3, three_ref))
    ]
    suffix = exact_dot(later[0], exact_dot(later[1], later[2])).T
    copies = []

    def write(time, chain):
        chain = chain.astype(jnp.bfloat16)
        width = held_ref.shape[2] // SPLIT
        for low in range(0, held_ref.shape[2], width):
            lanes = slice(low, low + width)
            staged_ref[time, :, lanes] = jnp.dot(
                chain, held_ref[time, :, lanes], preferred_element_type=jnp.float32
            ).astype(jnp.bfloat16)
            copies.append(
                pltpu.make_async_copy(
                    staged_ref.at[time, :, lanes], out_ref.at[time, :, lanes], sems.at[len(copies)]
                )
            )
            copies[-1].start()

    write(3, suffix)
    for k in range(3):
        write(2 - k, exact_dot(suffix, factors_ref[M * k : M * k + M, :], NT))
    for copy in copies:
        copy.wait()


SPLIT = 4


def smooth(later, factors, held):
    times = held.shape[0]
    return pl.pallas_call(
        smooth_kernel,
        in_specs=[VMEM] * 5,
        out_specs=HBM,
        out_shape=jax.ShapeDtypeStruct(held.shape, held.dtype),
        scratch_shapes=[pltpu.VMEM(held.shape, held.dtype), pltpu.SemaphoreType.DMA((times * SPLIT,))],
        compiler_params=pltpu.CompilerParams(vmem_limit_bytes=16 << 20),
        name="smooth",
    )(*later, factors, held)


XS, ZS, CORES = 4, 8, 2


def place(x, z, core):
    return ((x % XS) * ZS + z % ZS) * CORES + core % CORES


def sites():
    return [(x, z, c) for x in range(XS) for z in range(ZS) for c in range(CORES)]


def per_device(anomalies, obs_index, obs_weight):
    swap = [(place(*s), place(s[0], s[1], s[2] + 1)) for s in sites()]
    send, held, index_held, weight_held = gram_other(anomalies, obs_index, obs_weight)
    received = lax.ppermute(send, "space", swap)
    keep = gram_own(held, index_held, weight_held)
    part = keep + received
    for moves in (
        [lambda x, z: (x ^ 1, z)],
        [lambda x, z: (x, z ^ 1)],
        [lambda x, z: (x, z + 2), lambda x, z: (x, z + 6), lambda x, z: (x, z + 4)],
        [lambda x, z: (x ^ 2, z)],
    ):
        part = part + sum(
            lax.ppermute(part, "space", [(place(x, z, c), place(*move(x, z), c)) for x, z, c in sites()])
            for move in moves
        )
    own = weights_of(part)
    product, factors = products_of(own, lax.ppermute(own, "space", swap))
    later = [lax.ppermute(product, "tm", [(g, (g - k) % 4) for g in range(4)]) for k in (3, 2, 1)]
    later = [later[2], later[1], later[0]]
    return smooth(later, factors, held)


def solution(mesh):
    return jax.shard_map(
        per_device,
        mesh=mesh,
        in_specs=(P("tm", None, "space"), P("tm", "space"), P("tm", "space")),
        out_specs=P("tm", None, "space"),
        check_vma=False,
    )
```

```python
import jax
import jax.numpy as jnp
from jax import lax
from jax.experimental import pallas as pl
from jax.experimental.pallas import tpu as pltpu
from jax.sharding import PartitionSpec as P

M = 128
HALF = 64
LANES = 128
ROWS = 136
HIGHEST = lax.Precision.HIGHEST
NN = (((1,), (0,)), ((), ()))
NT = (((1,), (1,)), ((), ()))
TN = (((0,), (0,)), ((), ()))


def exact_dot(left, right, dims=NN):
    return lax.dot_general(left, right, dims, precision=HIGHEST, preferred_element_type=jnp.float32)


def iota(shape, dim):
    return lax.broadcasted_iota(jnp.int32, shape, dim)


def fold(gram):
    near = jnp.bitwise_and(iota((HALF, M), 1) - iota((HALF, M), 0), M - 1) < HALF
    across = iota((HALF, M), 1) == iota((HALF, M), 0) + HALF
    body = jnp.where(near, gram[:HALF], gram[HALF:])
    rest = jnp.sum(jnp.where(across, gram[:HALF], 0.0), axis=0, keepdims=True)
    return body, rest


def unfold(body, rest):
    near = jnp.bitwise_and(iota((HALF, M), 1) - iota((HALF, M), 0), M - 1) < HALF
    across = iota((HALF, M), 1) == iota((HALF, M), 0) + HALF
    diag = iota((M, M), 0) == iota((M, M), 1)
    top = jnp.where(near, body, jnp.where(across, jnp.broadcast_to(rest, (HALF, M)), 0.0))
    bottom = jnp.where(near, 0.0, body)
    half = jnp.concatenate([top, bottom], axis=0)
    return half + jnp.where(diag, 0.0, half.T)


def cell_scales(index, weight, blocks):
    count = index.shape[1]
    square = weight * weight
    first = square.astype(jnp.bfloat16).astype(jnp.float32)
    second = (square - first).astype(jnp.bfloat16).astype(jnp.float32)
    third = square - first - second
    high = lax.shift_right_logical(index, 7)
    low = jnp.bitwise_and(index, LANES - 1)
    in_block = iota((blocks, count), 0) == high
    rows = jnp.concatenate(
        [jnp.where(in_block, part, 0.0).astype(jnp.bfloat16) for part in (first, second, third)], axis=0
    )
    lanes = jnp.where(iota((LANES, count), 0) == low, 1.0, 0.0).astype(jnp.bfloat16)
    parts = lax.dot_general(rows, lanes, NT, preferred_element_type=jnp.float32)
    return jnp.sqrt(parts[:blocks] + parts[blocks : 2 * blocks] + parts[2 * blocks :])


def write_grams(first, held_ref, index_ref, weight_ref, part_ref, arrived):
    blocks = held_ref.shape[2] // LANES
    scales = [
        cell_scales(index_ref[pl.ds(first + k, 1), :], weight_ref[pl.ds(first + k, 1), :], blocks)
        for k in range(2)
    ]
    rests = []
    for k in range(2):
        arrived(k)
        scaled = jnp.concatenate(
            [
                (
                    held_ref[first + k, :, b * LANES : (b + 1) * LANES].astype(jnp.float32)
                    * scales[k][b : b + 1, :]
                ).astype(jnp.bfloat16)
                for b in range(blocks)
            ],
            axis=1,
        )
        gram = lax.dot_general(scaled, scaled, NT, preferred_element_type=jnp.float32)
        body, rest = fold(gram)
        part_ref[HALF * k : HALF * k + HALF, :] = body
        rests.append(jnp.broadcast_to(rest, (8, M)))
    row = iota((8, M), 0)
    part_ref[M:, :] = jnp.where(row == 0, rests[0], jnp.where(row == 1, rests[1], 0.0))


def gram_other_kernel(anomalies_ref, index_ref, weight_ref, part_ref, held_ref, index_held, weight_held, sems):
    core = lax.rem(lax.axis_index("space"), 2)
    order = [2 * (1 - core), 2 * (1 - core) + 1, 2 * core, 2 * core + 1]
    small = [
        pltpu.make_async_copy(index_ref, index_held, sems.at[0]),
        pltpu.make_async_copy(weight_ref, weight_held, sems.at[1]),
    ]
    large = [
        pltpu.make_async_copy(anomalies_ref.at[t], held_ref.at[t], sems.at[2 + k]) for k, t in enumerate(order)
    ]
    for copy in small + large:
        copy.start()
    for copy in small:
        copy.wait()
    write_grams(order[0], held_ref, index_held, weight_held, part_ref, lambda k: large[k].wait())
    for copy in large[2:]:
        copy.wait()


def gram_own_kernel(held_ref, index_ref, weight_ref, part_ref):
    core = lax.rem(lax.axis_index("space"), 2)
    write_grams(2 * core, held_ref, index_ref, weight_ref, part_ref, lambda k: None)


HBM = pl.BlockSpec(memory_space=pltpu.HBM)
VMEM = pl.BlockSpec(memory_space=pltpu.VMEM)


def gram_cost(anomalies):
    times, members, cells = anomalies.shape
    return pl.CostEstimate(
        flops=times * members * members * cells, bytes_accessed=times * members * cells, transcendentals=0
    )


def gram_other(anomalies, obs_index, obs_weight):
    inputs = (anomalies, obs_index, obs_weight)
    return pl.pallas_call(
        gram_other_kernel,
        in_specs=[HBM] * 3,
        out_specs=[VMEM] * 4,
        out_shape=[
            jax.ShapeDtypeStruct((ROWS, M), jnp.float32),
            *(jax.ShapeDtypeStruct(x.shape, x.dtype) for x in inputs),
        ],
        scratch_shapes=[pltpu.SemaphoreType.DMA((6,))],
        compiler_params=pltpu.CompilerParams(vmem_limit_bytes=12 << 20),
        cost_estimate=gram_cost(anomalies),
        name="gram_other",
    )(*(pltpu.with_memory_space_constraint(x, pltpu.HBM) for x in inputs))


def gram_own(held, obs_index, obs_weight):
    return pl.pallas_call(
        gram_own_kernel,
        in_specs=[VMEM] * 3,
        out_specs=VMEM,
        out_shape=jax.ShapeDtypeStruct((ROWS, M), jnp.float32),
        compiler_params=pltpu.CompilerParams(vmem_limit_bytes=12 << 20),
        cost_estimate=gram_cost(held),
        name="gram_own",
    )(held, obs_index, obs_weight)


def invert_four(at):
    e11, e12, e22 = at(0, 0), at(0, 1), at(1, 1)
    f11, f12, f21, f22 = at(0, 2), at(0, 3), at(1, 2), at(1, 3)
    h11, h12, h22 = at(2, 2), at(2, 3), at(3, 3)
    d = 1.0 / (e11 * e22 - e12 * e12)
    x11, x12 = (e22 * f11 - e12 * f21) * d, (e22 * f12 - e12 * f22) * d
    x21, x22 = (e11 * f21 - e12 * f11) * d, (e11 * f22 - e12 * f12) * d
    s11 = h11 - (f11 * x11 + f21 * x21)
    s12 = h12 - (f11 * x12 + f21 * x22)
    s22 = h22 - (f12 * x12 + f22 * x22)
    g = 1.0 / (s11 * s22 - s12 * s12)
    m33, m34, m44 = s22 * g, -s12 * g, s11 * g
    m13, m14 = -(x11 * m33 + x12 * m34), -(x11 * m34 + x12 * m44)
    m23, m24 = -(x21 * m33 + x22 * m34), -(x21 * m34 + x22 * m44)
    m11 = e22 * d - (m13 * x11 + m14 * x12)
    m12 = -e12 * d - (m13 * x21 + m14 * x22)
    m22 = e11 * d - (m23 * x21 + m24 * x22)
    return (
        (m11, m12, m13, m14),
        (m12, m22, m23, m24),
        (m13, m23, m33, m34),
        (m14, m24, m34, m44),
    )


def weighted(line, values):
    return (line[0] * values[0] + line[1] * values[1]) + (line[2] * values[2] + line[3] * values[3])


def invert_halves(panels):
    lane = iota((8, LANES), 1)
    column = jnp.bitwise_and(lane, HALF - 1)
    first_lane = lane - column
    row = iota((8, LANES), 0)

    def column_of(panel, k):
        return jnp.take_along_axis(panel, first_lane + k, axis=1)

    def row_of(panel, k):
        return jnp.broadcast_to(panel[k : k + 1, :], panel.shape)

    def solve(panel, start, offset, inverse):
        pivots = (column >= start) & (column < start + 4)
        rows = [
            jnp.where(pivots, jnp.where(column == start + j, 1.0, 0.0), row_of(panel, offset + j)) for j in range(4)
        ]
        return pivots, [weighted(line, rows) for line in inverse]

    def eliminate(panel, pivots, columns, solved):
        out = jnp.where(pivots, 0.0, panel)
        return out - weighted(columns, solved)

    def place_rows(panel, offset, solved):
        for i in range(4):
            panel = jnp.where(row == offset + i, solved[i], panel)
        return panel

    count = len(panels)
    for own in range(count):
        start = 8 * own
        columns = [column_of(panels[own], start + k) for k in range(8)]
        inverse = invert_four(lambda i, j: row_of(columns[j], i))
        pivots, solved = solve(panels[own], start, 0, inverse)
        ahead = [
            [weighted(line, [row_of(columns[k], l) for l in range(4)]) for line in inverse] for k in range(4, 8)
        ]
        later = [columns[4 + k] - weighted(columns[:4], ahead[k]) for k in range(4)]
        second = invert_four(lambda i, j: row_of(later[j], 4 + i))
        current = place_rows(eliminate(panels[own], pivots, columns[:4], solved), 0, solved)
        pivots_two, solved_two = solve(current, start + 4, 4, second)
        result = list(panels)
        for p in [(own + 1 + q) % count for q in range(count - 1)]:
            near = [column_of(panels[p], start + j) for j in range(4)]
            far = [column_of(panels[p], start + 4 + k) - weighted(near, ahead[k]) for k in range(4)]
            out = eliminate(panels[p], pivots, near, solved)
            result[p] = eliminate(out, pivots_two, far, solved_two)
        far = [column_of(current, start + 4 + k) for k in range(4)]
        result[own] = place_rows(eliminate(current, pivots_two, far, solved_two), 4, solved_two)
        panels = result
    return panels


def invert_packed(packed):
    return jnp.concatenate(invert_halves([packed[8 * p : 8 * p + 8] for p in range(8)]), axis=0)


def invert_pair(pair):
    left = iota((HALF, M), 1) < HALF
    corner = iota((HALF, M), 1) == iota((HALF, M), 0) + HALF
    one, two = pair
    first = invert_packed(jnp.where(left, one[:HALF], pltpu.roll(two[:HALF], HALF, 1)))
    firsts = (first, pltpu.roll(first, HALF, 1))
    crosses = [exact_dot(g[HALF:, :HALF], f[:, :HALF]) for g, f in zip(pair, firsts)]
    schur = [g[HALF:] - exact_dot(x, g[:HALF]) for g, x in zip(pair, crosses)]
    changes = [exact_dot(s[:, :HALF], f[:, :HALF]) for s, f in zip(schur, firsts)]
    schur = [s - exact_dot(x, g[:HALF]) for s, x, g in zip(schur, changes, pair)]
    crosses = [x + change for x, change in zip(crosses, changes)]
    second = invert_packed(jnp.where(left, pltpu.roll(schur[0], HALF, 1), schur[1]))
    seconds = (second, pltpu.roll(second, HALF, 1))
    inverses = []
    for f, x, s in zip(firsts, crosses, seconds):
        border = jnp.concatenate([x, jnp.zeros((HALF, HALF), jnp.float32)], axis=1) - jnp.where(corner, 1.0, 0.0)
        whole = exact_dot(border, exact_dot(s[:, :HALF], border), TN)
        inverses.append(jnp.concatenate([whole[:HALF] + jnp.where(left, f, 0.0), whole[HALF:]], axis=0))
    return inverses


def weights_kernel(total_ref, out_ref):
    dof = float(M - 1)
    total = total_ref[...]
    diag = jnp.where(iota((M, M), 0) == iota((M, M), 1), dof, 0.0)
    pair = [
        unfold(total[HALF * k : HALF * k + HALF], total[M + k : M + k + 1]) + diag for k in range(2)
    ]
    first, second = (dof * w for w in invert_pair(pair))
    out_ref[:M, :] = second
    out_ref[M:, :] = exact_dot(first, second)


def weights_of(total):
    return pl.pallas_call(
        weights_kernel,
        out_shape=jax.ShapeDtypeStruct((2 * M, M), jnp.float32),
        compiler_params=pltpu.CompilerParams(vmem_limit_bytes=4 << 20),
        name="weights",
    )(total)


def products_kernel(own_ref, other_ref, product_ref, factors_ref):
    core = lax.rem(lax.axis_index("space"), 2)
    own, other = own_ref[...], other_ref[...]
    early = jnp.where(core == 0, own, other)
    late = jnp.where(core == 0, other, own)
    product_ref[...] = exact_dot(early[M:], late[M:])
    factors_ref[: 2 * M, :] = late
    factors_ref[2 * M :, :] = exact_dot(early[:M], late[M:])


def products_of(own, other):
    return pl.pallas_call(
        products_kernel,
        out_shape=[
            jax.ShapeDtypeStruct((M, M), jnp.float32),
            jax.ShapeDtypeStruct((3 * M, M), jnp.float32),
        ],
        compiler_params=pltpu.CompilerParams(vmem_limit_bytes=4 << 20),
        name="products",
    )(own, other)


def smooth_kernel(one_ref, two_ref, three_ref, factors_ref, held_ref, out_ref, staged_ref, sems):
    position = lax.axis_index("tm")
    eye = jnp.where(iota((M, M), 0) == iota((M, M), 1), 1.0, 0.0)
    core = lax.rem(lax.axis_index("space"), 2)
    one = jnp.where(core == 0, one_ref[...], three_ref[...])
    three = jnp.where(core == 0, three_ref[...], one_ref[...])
    later = [jnp.where(position + k < 4, x, eye) for k, x in ((1, one), (2, two_ref[...]), (3, three))]
    suffix = exact_dot(later[0], exact_dot(later[1], later[2])).T
    copies = []

    def write(time, chain):
        chain = chain.astype(jnp.bfloat16)
        width = held_ref.shape[2] // SPLIT
        for low in range(0, held_ref.shape[2], width):
            lanes = slice(low, low + width)
            staged_ref[time, :, lanes] = jnp.dot(
                chain, held_ref[time, :, lanes], preferred_element_type=jnp.float32
            ).astype(jnp.bfloat16)
            copies.append(
                pltpu.make_async_copy(
                    staged_ref.at[time, :, lanes], out_ref.at[time, :, lanes], sems.at[len(copies)]
                )
            )
            copies[-1].start()

    write(3, suffix)
    for k in range(3):
        write(2 - k, exact_dot(suffix, factors_ref[M * k : M * k + M, :], NT))
    for copy in copies:
        copy.wait()


SPLIT = 4


def smooth(later, factors, held):
    times = held.shape[0]
    return pl.pallas_call(
        smooth_kernel,
        in_specs=[VMEM] * 5,
        out_specs=HBM,
        out_shape=jax.ShapeDtypeStruct(held.shape, held.dtype),
        scratch_shapes=[pltpu.VMEM(held.shape, held.dtype), pltpu.SemaphoreType.DMA((times * SPLIT,))],
        compiler_params=pltpu.CompilerParams(vmem_limit_bytes=16 << 20),
        name="smooth",
    )(*later, factors, held)


XS, ZS, CORES = 4, 8, 2


def place(x, z, core):
    return ((x % XS) * ZS + z % ZS) * CORES + core % CORES


def sites():
    return [(x, z, c) for x in range(XS) for z in range(ZS) for c in range(CORES)]


def per_device(anomalies, obs_index, obs_weight):
    swap = [(place(*s), place(s[0], s[1], s[2] + 1)) for s in sites()]
    send, held, index_held, weight_held = gram_other(anomalies, obs_index, obs_weight)
    received = lax.ppermute(send, "space", swap)
    keep = gram_own(held, index_held, weight_held)
    part = keep + received
    for moves in (
        [lambda x, z: (x ^ 1, z), lambda x, z: (x, z ^ 1), lambda x, z: (x ^ 1, z ^ 1)],
        [lambda x, z: (x ^ 2, z), lambda x, z: (x, z ^ 2), lambda x, z: (x ^ 2, z ^ 2)],
        [lambda x, z: (x, z ^ 4)],
    ):
        part = part + sum(
            lax.ppermute(part, "space", [(place(x, z, c), place(*move(x, z), c)) for x, z, c in sites()])
            for move in moves
        )
    own = weights_of(part)
    product, factors = products_of(own, lax.ppermute(own, "space", swap))
    sides = [
        (g * len(sites()) + place(*s), (g - (1 if s[2] == 0 else 3)) % 4 * len(sites()) + place(*s))
        for g in range(4)
        for s in sites()
    ]
    second = lax.ppermute(product, "tm", [(g, (g - 2) % 4) for g in range(4)])
    near = lax.ppermute(product, ("tm", "space"), sides)
    far = lax.ppermute(near, "space", swap)
    later = [near, second, far]
    return smooth(later, factors, held)


def solution(mesh):
    return jax.shard_map(
        per_device,
        mesh=mesh,
        in_specs=(P("tm", None, "space"), P("tm", "space"), P("tm", "space")),
        out_specs=P("tm", None, "space"),
        check_vma=False,
    )
```
